32 devices in a mesh: dom: 16 (over z, y, x), spin: 2 (over core).
Axes of the slice: x: 2, y: 2, z: 4, core: 2. Of those that a mesh axis runs over, the one named last changes fastest.
Arguments:
- vectors: float32 [2, 8, 262144], P('spin', None, 'dom'), may hold values from -17 to 17
- basis: float32 [2, 16, 262144], P('spin', None, 'dom'), may hold values from -17 to 17
- potential: float32 [2, 262144], P('spin', 'dom'), may hold values from 1 to 3
- hop_table: bfloat16 [8, 128, 128], replicated, may hold values from -0.25 to 0.25
- soc_table: bfloat16 [2, 128, 128], replicated, may hold values from -0.5 to 0.5
- nbr_block: int32 [2048, 16], P('dom'), may hold values from 0 to 2047, as said below
- nbr_type: int32 [2048, 16], P('dom'), may hold values from 0 to 7
- nbr_count: int32 [2048], P('dom'), may hold values from 1 to 16, as said below
- flip_block: int32 [2048], P('dom'), may hold values from 0 to 2047, as said below
Outputs:
- block_one: float32 [2, 8, 262144], P('spin', None, 'dom')
- block_two: float32 [2, 8, 262144], P('spin', None, 'dom')
- coefs_one: float32 [32, 8], replicated
- coefs_two: float32 [40, 8], replicated
The draws below stay inside these ranges and needn't reach their ends.
Inputs may be any that keep to these rules, and one draw needn't show every extreme that they name: nbr_block[i, l] equals i + d modulo 2048 with -8 <= d <= 8; slots at or beyond nbr_count[i] are ignored; in slot 0, the first block of each group of 128 has d = -8 and the last has d = 8. `nbr_count`: some block has all 16 slots live. flip_block[i] lies in the same domain as i: flip_block[i] // 128 == i // 128.
All inputs are finite; a program needn't handle non-finite values.
Results may differ from the reference program's by a relative error of at most 0.0033.
Values may be sent and summed in bfloat16 or wider, within the bound.
A program may use at most 64 MiB of HBM per device.

```python
import math
import jax
import jax.numpy as jnp
from jax import lax

B = 128
K = 8
NB_DEV = 128
RANGE = 8
NTYPES = 8
MAXNB = 16
M = 16
NBLK = 2048
NORB = 262144


def orbital_scale(key, shape):
    spread = jax.random.uniform(key, shape, jnp.float32)
    return jnp.exp(spread * math.log(10.0)) / math.sqrt(99.0 / (2.0 * math.log(10.0)))


def draw_vectors(key, part):
    key_base, key_scale, key_column = jax.random.split(key, 3)
    base_values = jnp.clip(jax.random.normal(key_base, (2, K, NORB), jnp.float32), -6.0, 6.0)
    column_scale = jnp.exp(jax.random.uniform(key_column, (1, K, 1), jnp.float32, math.log(0.8), math.log(1.25)))
    return (base_values * column_scale * orbital_scale(key_scale, (2, 1, NORB))).astype(jnp.float32)


def draw_basis(key, part):
    key_base, key_scale, key_common = jax.random.split(key, 3)
    base_values = jnp.clip(jax.random.normal(key_base, (2, M, NORB), jnp.float32), -6.0, 6.0)
    shared_part = jnp.clip(jax.random.normal(key_common, (2, 1, NORB), jnp.float32), -6.0, 6.0)
    mixed_values = (base_values + 0.23 * shared_part) / math.sqrt(1.0529)
    return (mixed_values * orbital_scale(key_scale, (2, 1, NORB))).astype(jnp.float32)


def draw_nbr_block(key, part):
    block_rows = jnp.arange(NBLK, dtype=jnp.int32)[:, None]
    offset = jax.random.randint(key, (NBLK, MAXNB), -RANGE, RANGE + 1, dtype=jnp.int32)
    local_pos = block_rows % NB_DEV
    slot_zero = jnp.arange(MAXNB, dtype=jnp.int32)[None, :] == 0
    offset = jnp.where(slot_zero & (local_pos == 0), -RANGE, offset)
    offset = jnp.where(slot_zero & (local_pos == NB_DEV - 1), RANGE, offset)
    return ((block_rows + offset) % NBLK).astype(jnp.int32)


def draw_nbr_count(key, part):
    key_heavy, key_pick, key_row, key_count = jax.random.split(jax.random.fold_in(key, 17), 4)
    domain_total = NBLK // NB_DEV
    heavy_domain = jax.random.randint(key_heavy, (domain_total,), 0, 8, dtype=jnp.int32) == 0
    chosen_domain = jax.random.randint(key_pick, (), 0, domain_total, dtype=jnp.int32)
    heavy_domain = heavy_domain | (jnp.arange(domain_total, dtype=jnp.int32) == chosen_domain)
    slot_cap = jnp.where(heavy_domain, MAXNB, max(MAXNB // 4, 1)).astype(jnp.int32)
    cap_rows = jnp.repeat(slot_cap, NB_DEV)
    live_count = jax.random.randint(key_count, (NBLK,), 1, cap_rows + 1, dtype=jnp.int32)
    full_row = chosen_domain * NB_DEV + jax.random.randint(key_row, (), 0, NB_DEV, dtype=jnp.int32)
    live_count = jnp.where(jnp.arange(NBLK, dtype=jnp.int32) == full_row, MAXNB, live_count)
    return live_count.astype(jnp.int32)


def draw_flip_block(key, part):
    block_rows = jnp.arange(NBLK, dtype=jnp.int32)
    domain_start = block_rows // NB_DEV * NB_DEV
    return (domain_start + jax.random.randint(key, (NBLK,), 0, NB_DEV, dtype=jnp.int32)).astype(jnp.int32)


def with_ends(result, key, least, high):
    dims = result.shape
    spot = [jax.random.randint(jax.random.fold_in(key, axis), (), 0, dims[axis]) for axis in range(len(dims))]
    result = result.at[tuple(spot)].set(least)
    longest = dims.index(max(dims))
    spot[longest] = (spot[longest] + 1) % dims[longest]
    return result.at[tuple(spot)].set(high)


def block_scale(rng, dims, cuts, smallest, largest):
    loudness = 1.0
    for axis_at, shards_of in cuts:
        draws = jax.random.uniform(jax.random.fold_in(jax.random.fold_in(rng, 6), axis_at), (shards_of,), jnp.float32, smallest / len(cuts), largest / len(cuts))
        loudness = loudness * jnp.repeat(jnp.exp(draws), dims[axis_at] // shards_of).reshape((-1,) + (1,) * (len(dims) - 1 - axis_at))
    return loudness


def noise(rng, dims, scale, reach, kind=jnp.bfloat16):
    entries = jax.random.normal(rng, dims, jnp.float32) * scale
    return jnp.minimum(jnp.maximum(entries, -reach), reach).astype(kind)


def setup_inputs(seed: int = 0) -> dict:
    key_of = jax.random.split(jax.random.key(seed), 10)
    vectors = draw_vectors(jax.random.fold_in(key_of[9], 71), 0)
    basis = draw_basis(jax.random.fold_in(key_of[9], 71), 0)
    potential = jnp.clip(1.0 + 2.0 * jax.random.uniform(key_of[2], (2, NORB), jnp.float32) ** block_scale(key_of[2], (2, NORB), ((0, 2), (1, 16)), -0.2, 0.2), 1.0, 3.0)
    hop_table = noise(key_of[3], (NTYPES, B, B), (4 * B) ** -0.5, 0.25)
    soc_table = noise(key_of[4], (2, B, B), B ** -0.5, 0.5)
    nbr_block = draw_nbr_block(jax.random.fold_in(key_of[9], 71), 0)
    nbr_type = with_ends(jax.random.randint(key_of[6], (NBLK, MAXNB), 0, NTYPES), jax.random.fold_in(key_of[6], 1), 0, NTYPES - 1).astype(jnp.int32)
    nbr_count = draw_nbr_count(jax.random.fold_in(key_of[9], 71), 0)
    flip_block = draw_flip_block(jax.random.fold_in(key_of[9], 71), 0)
    return dict(vectors=vectors, basis=basis, potential=potential, hop_table=hop_table, soc_table=soc_table, nbr_block=nbr_block, nbr_type=nbr_type, nbr_count=nbr_count, flip_block=flip_block)


def hopping_image(rounded, hop_table, nbr_block, nbr_type, nbr_count):
    block_total = rounded.shape[2]
    domain_count = block_total // NB_DEV
    wrapped = jnp.concatenate([rounded[:, :, block_total - RANGE:], rounded, rounded[:, :, :RANGE]], axis=2)
    table_f32 = hop_table.astype(jnp.float32)
    local_index = jnp.arange(NB_DEV, dtype=jnp.int32)
    slot_index = jnp.arange(MAXNB, dtype=jnp.int32)

    def one_domain(domain):
        first_block = (domain * NB_DEV).astype(jnp.int32)
        extended = lax.dynamic_slice_in_dim(wrapped, first_block, NB_DEV + 2 * RANGE, 2).astype(jnp.float32)
        products = jnp.einsum('skjc,tbc->skjtb', extended, table_f32, precision=lax.Precision.HIGHEST)
        products = products.reshape(2, K, (NB_DEV + 2 * RANGE) * NTYPES, B)
        neighbours = lax.dynamic_slice_in_dim(nbr_block, first_block, NB_DEV, 0)
        types_here = lax.dynamic_slice_in_dim(nbr_type, first_block, NB_DEV, 0)
        counts_here = lax.dynamic_slice_in_dim(nbr_count, first_block, NB_DEV, 0)
        global_rows = first_block + local_index
        offset = (neighbours - global_rows[:, None] + RANGE) % block_total - RANGE
        flat_index = ((local_index[:, None] + RANGE + offset) * NTYPES + types_here).astype(jnp.int32)
        live_mask = (slot_index[None, :] < counts_here[:, None]).astype(jnp.float32)
        gathered = jnp.take(products, flat_index.reshape(-1), axis=2).reshape(2, K, NB_DEV, MAXNB, B)
        return jnp.sum(gathered * live_mask[None, None, :, :, None], axis=3)
    pieces = lax.map(one_domain, jnp.arange(domain_count, dtype=jnp.int32))
    return jnp.moveaxis(pieces, 0, 2).reshape(2, K, block_total, B)

def apply_operator(field, potential, hop_table, soc_table, nbr_block, nbr_type, nbr_count, flip_block):
    block_total = field.shape[2] // B
    rounded = field.reshape(2, K, block_total, B).astype(jnp.bfloat16)
    hopping = hopping_image(rounded, hop_table, nbr_block, nbr_type, nbr_count)
    other_side = jnp.take(rounded[::-1], flip_block, axis=2).astype(jnp.float32)
    flip_term = jnp.einsum('skic,sbc->skib', other_side, soc_table.astype(jnp.float32), precision=lax.Precision.HIGHEST)
    return potential[:, None, :] * field + (hopping + flip_term).reshape(2, K, -1)

def orthonormal(span, image):
    norm_count = float(2 * image.shape[2])
    highest = lax.Precision.HIGHEST
    first_coef = jnp.einsum('smn,skn->mk', span, image, precision=highest) / norm_count
    once = image - jnp.einsum('smn,mk->skn', span, first_coef, precision=highest)
    second_coef = jnp.einsum('smn,skn->mk', span, once, precision=highest) / norm_count
    twice = once - jnp.einsum('smn,mk->skn', span, second_coef, precision=highest)
    gram_matrix = jnp.einsum('skn,sln->kl', twice, twice, precision=highest) / norm_count
    lower_factor = jnp.linalg.cholesky(gram_matrix)
    rows_form = jnp.transpose(twice, (1, 0, 2)).reshape(K, -1)
    solved = lax.linalg.triangular_solve(lower_factor, rows_form, left_side=True, lower=True)
    new_block = jnp.transpose(solved.reshape(K, 2, -1), (1, 0, 2))
    coefs = jnp.concatenate([first_coef + second_coef, lower_factor.T], axis=0)
    return (new_block, coefs)

def reference(vectors, basis, potential, hop_table, soc_table, nbr_block, nbr_type, nbr_count, flip_block):
    image = apply_operator(vectors, potential, hop_table, soc_table, nbr_block, nbr_type, nbr_count, flip_block)
    span = jnp.concatenate([basis, vectors], axis=1)
    block_one, coefs_one = orthonormal(span, image)
    image_two = apply_operator(block_one, potential, hop_table, soc_table, nbr_block, nbr_type, nbr_count, flip_block)
    span_two = jnp.concatenate([span, block_one], axis=1)
    block_two, coefs_two = orthonormal(span_two, image_two)
    return (block_one, block_two, coefs_one, coefs_two)
```

```python
import functools
import jax
import jax.numpy as jnp
from jax import lax
from jax.experimental import pallas as pl
from jax.experimental.pallas import tpu as pltpu
from jax.sharding import PartitionSpec as P

RANGE = 8
MESH = pl.DeviceIdType.MESH
NT = (((1,), (1,)), ((), ()))
NN = (((1,), (0,)), ((), ()))


def high_dot(left, right, dims):
    return lax.dot_general(
        left, right, dims, precision=lax.Precision.HIGHEST, preferred_element_type=jnp.float32
    )


def kernel(
    cfg,
    vec_ref, basis_ref, pot_ref, hop_ref, soc_ref, idx_ref,
    one_ref, two_ref, coef_one_ref, coef_two_ref,
    ext_ref, other_ref, halo_ref, prod_ref, image_ref, bcast_ref, stage_a_ref, stage_b_ref,
    link_send, link_recv, a_send, a_recv, b_send, b_recv,
):
    dom_total, group_doms, blocks, width, types, slots, vecs, kept, norm = cfg
    groups = dom_total // group_doms
    group_size = 2 * group_doms
    dom, spin = lax.axis_index("dom"), lax.axis_index("spin")
    rank_a = (dom % group_doms) * 2 + spin
    rank_b = dom // group_doms
    dom_base = rank_b * group_doms
    left, right = (dom + dom_total - 1) % dom_total, (dom + 1) % dom_total
    rows = blocks * vecs
    halo_rows = RANGE * vecs
    reach = blocks + 2 * RANGE
    zero_tile = reach * types
    flip_base = zero_tile + 1

    def peer_a(shift):
        other = (rank_a + shift) % group_size
        return (dom_base + other // 2, other % 2)

    def peer_b(shift):
        return (((rank_b + shift) % groups) * group_doms + dom % group_doms, spin)

    barrier = pltpu.get_barrier_semaphore()
    for shift in range(1, group_size):
        pl.semaphore_signal(barrier, inc=1, device_id=peer_a(shift), device_id_type=MESH)
    for shift in range(1, groups):
        pl.semaphore_signal(barrier, inc=1, device_id=peer_b(shift), device_id_type=MESH)
    for side in (left, right):
        pl.semaphore_signal(barrier, inc=1, device_id=(side, spin), device_id_type=MESH)

    lane = lax.broadcasted_iota(jnp.int32, (vecs, width), 1)
    row = lax.broadcasted_iota(jnp.int32, (vecs, width), 0)

    def cols(tile):
        return pl.ds(pl.multiple_of(tile * width, width), width)

    def link_copies(app):
        ext, halo = ext_ref.at[app], halo_ref.at[app]
        tail = pltpu.make_async_remote_copy(
            src_ref=ext.at[pl.ds(rows - halo_rows, halo_rows)],
            dst_ref=halo.at[pl.ds(0, halo_rows)],
            send_sem=link_send.at[app, 0], recv_sem=link_recv.at[app, 0],
            device_id=(right, spin), device_id_type=MESH)
        head = pltpu.make_async_remote_copy(
            src_ref=ext.at[pl.ds(0, halo_rows)],
            dst_ref=halo.at[pl.ds(halo_rows, halo_rows)],
            send_sem=link_send.at[app, 1], recv_sem=link_recv.at[app, 1],
            device_id=(left, spin), device_id_type=MESH)
        flip = pltpu.make_async_remote_copy(
            src_ref=ext, dst_ref=other_ref.at[app],
            send_sem=link_send.at[app, 2], recv_sem=link_recv.at[app, 2],
            device_id=(dom, 1 - spin), device_id_type=MESH)
        return tail, head, flip

    def gram_rows(left_ref, sources):
        count = sum(hi for _, hi in sources)

        def body(tile, sums):
            ours = left_ref[:, cols(tile)]
            picked = [ref[pl.ds(m, 1), cols(tile)] for ref, hi in sources for m in range(hi)]
            return tuple(total + ours * one for total, one in zip(sums, picked))

        sums = lax.fori_loop(
            0, blocks, body, tuple(jnp.zeros((vecs, width), jnp.float32) for _ in range(count)),
            unroll=2)
        out = jnp.zeros((vecs, width), jnp.float32)
        for m, total in enumerate(sums):
            out = jnp.where(lane == m, jnp.sum(total, axis=1, keepdims=True), out)
        return out

    def products(source, count, first):
        def body(pair, carry):
            weights = hop_ref[pl.ds(pl.multiple_of(pair * 2 * width, 2 * width), 2 * width), :]
            out = lax.dot_general(source[...], weights, NT, preferred_element_type=jnp.float32)
            for half in range(2):
                part = out[:, half * width:(half + 1) * width].reshape(count, vecs, width)
                prod_ref[pl.ds((pair * 2 + half) * reach + first, count)] = part
            return carry
        lax.fori_loop(0, types // 2, body, 0)

    def flip_products(app):
        out = lax.dot_general(
            other_ref[app], soc_ref[spin], NT, preferred_element_type=jnp.float32)
        prod_ref[pl.ds(flip_base, blocks)] = out.reshape(blocks, vecs, width)

    def gather(field_ref, low, high):
        def body(block, carry):
            terms = [pot_ref[pl.ds(0, 1), cols(block)] * field_ref[:, cols(block)]]
            for slot in range(slots + 1):
                terms.append(prod_ref[idx_ref[block * (slots + 1) + slot]])
            while len(terms) > 1:
                terms = [sum(terms[p:p + 2][1:], terms[p]) for p in range(0, len(terms), 2)]
            image_ref[:, cols(block)] = terms[0]
            return carry
        lax.fori_loop(low, high, body, 0, unroll=2)

    def share(app, value):
        def stage(ref, send, recv, rank, size, peer, mine):
            ref[app, rank] = mine
            def copy(shift, slot):
                return pltpu.make_async_remote_copy(
                    src_ref=ref.at[app, rank], dst_ref=ref.at[app, slot],
                    send_sem=send.at[app, shift], recv_sem=recv.at[app, slot],
                    device_id=peer(shift), device_id_type=MESH)
            for shift in range(1, size):
                copy(shift, rank).start()
            for shift in range(1, size):
                copy(shift, (rank + size - shift) % size).wait_recv()
            for shift in range(1, size):
                copy(shift, rank).wait_send()
            total = ref[app, 0]
            for slot in range(1, size):
                total = total + ref[app, slot]
            return total
        value = stage(stage_a_ref, a_send, a_recv, rank_a, group_size, peer_a, value)
        if groups > 1:
            value = stage(stage_b_ref, b_send, b_recv, rank_b, groups, peer_b, value)
        return value * (1.0 / norm)

    def lanes(value, start, count):
        moved = value if start == 0 else pltpu.roll(value, width - start, 1)
        return jnp.where(lane < count, moved, 0.0)

    def tall(pieces):
        pad = width - vecs * len(pieces)
        return jnp.concatenate(list(pieces) + [jnp.zeros((pad, width), jnp.float32)], axis=0)

    def factor(first_t, image_gram, span_gram, span_count):
        total_t = 2.0 * first_t - high_dot(first_t, span_gram, NT)
        moved = high_dot(total_t, span_gram, NT) - first_t
        gram = image_gram + high_dot(moved, tall([total_t]), NT) - high_dot(total_t, tall([first_t]), NT)
        table = jnp.where(lane < vecs, gram, jnp.where(lane == row + vecs, 1.0, 0.0))
        table = table - pltpu.roll(total_t, 2 * vecs, 1)
        for j in range(vecs):
            column = jnp.broadcast_to(table[:, j:j + 1], (vecs, width))
            pivot_row = jnp.broadcast_to(table[j:j + 1, :], (vecs, width))
            pivot = jnp.broadcast_to(column[j:j + 1, :], (vecs, width))
            scale = 1.0 / jnp.sqrt(pivot)
            pivot_row = pivot_row * scale
            table = jnp.where(
                row == j, pivot_row, jnp.where(row > j, table - column * scale * pivot_row, table))
        upper = jnp.where((lane >= row) & (lane < vecs), table, 0.0)
        for m in range(vecs + span_count):
            bcast_ref[m] = jnp.broadcast_to(table[:, vecs + m:vecs + m + 1], (vecs, width))
        return total_t + pltpu.roll(upper, 64, 1)

    def combine(sources, out_ref, ext_out):
        step = 4

        def body(chunk, carry):
            sums = [None] * step
            m = 0
            for ref, hi in sources:
                for r in range(hi):
                    coef = bcast_ref[m]
                    for u in range(step):
                        term = coef * ref[pl.ds(r, 1), cols(chunk * step + u)]
                        sums[u] = term if sums[u] is None else sums[u] + term
                    m += 1
            for u in range(step):
                out_ref[:, cols(chunk * step + u)] = sums[u]
            if ext_out is not None:
                for u in range(0, step, 2):
                    pair = jnp.concatenate(sums[u:u + 2], axis=0).astype(jnp.bfloat16)
                    at = pl.multiple_of((chunk * step + u) * vecs, 2 * vecs)
                    ext_out[pl.ds(at, 2 * vecs), :] = pair
            return carry
        return step, body

    field, basis = vec_ref.at[0], basis_ref.at[0]
    one, two = one_ref.at[0], two_ref.at[0]

    def round_body(pair, carry):
        both = jnp.concatenate([field[:, cols(2 * pair)], field[:, cols(2 * pair + 1)]], axis=0)
        ext_ref[0, pl.ds(pl.multiple_of(pair * 2 * vecs, 2 * vecs), 2 * vecs), :] = both.astype(
            jnp.bfloat16)
        return carry

    lax.fori_loop(0, blocks // 2, round_body, 0, unroll=4)
    prod_ref[zero_tile] = jnp.zeros((vecs, width), jnp.float32)
    low_gram = [gram_rows(basis.at[pl.ds(g * vecs, vecs)], [(basis, (g + 1) * vecs)])
                for g in range(kept // vecs)]
    low_gram.append(gram_rows(field, [(basis, kept), (field, vecs)]))
    pl.semaphore_wait(barrier, group_size - 1 + groups - 1 + 2)

    def apply_and_gram(app, field_ref, extra, sources):
        tail, head, flip = link_copies(app)
        products(ext_ref.at[app], blocks, 0)
        early = extra()
        flip.wait_recv()
        flip_products(app)
        gather(field_ref, RANGE, blocks - RANGE)
        tail.wait_recv()
        head.wait_recv()
        products(halo_ref.at[app], 2 * RANGE, blocks)
        gather(field_ref, 0, RANGE)
        gather(field_ref, blocks - RANGE, blocks)
        result = gram_rows(image_ref, sources + [(image_ref, vecs)])
        tail.wait_send()
        head.wait_send()
        flip.wait_send()
        return result, early

    for copy in link_copies(0):
        copy.start()
    span_one = kept + vecs
    result, _ = apply_and_gram(0, field, lambda: None, [(basis, kept), (field, vecs)])
    packed = result
    at = span_one + vecs
    for g in range(span_one // vecs):
        packed = packed + pltpu.roll(low_gram[g], at, 1)
        at += (g + 1) * vecs
    packed = share(0, packed)
    pieces = []
    at = span_one + vecs
    for g in range(span_one // vecs):
        pieces.append(lanes(packed, at, (g + 1) * vecs))
        at += (g + 1) * vecs
    low = tall(pieces)
    wide_row = lax.broadcasted_iota(jnp.int32, (width, width), 0) // vecs
    wide_lane = lax.broadcasted_iota(jnp.int32, (width, width), 1) // vecs
    span_gram = low + jnp.where(wide_row < wide_lane, low.T, 0.0)
    coef_one_ref[...] = factor(
        lanes(packed, 0, span_one), lanes(packed, span_one, vecs), span_gram, span_one)

    step, body = combine([(image_ref, vecs), (basis, kept), (field, vecs)], one, ext_ref.at[1])
    chunks, edge = blocks // step, RANGE // step
    tail, head, flip = link_copies(1)
    lax.fori_loop(0, edge, body, 0)
    lax.fori_loop(chunks - edge, chunks, body, 0)
    tail.start()
    head.start()
    lax.fori_loop(edge, chunks - edge, body, 0)
    flip.start()

    span_two = span_one + vecs
    result, early = apply_and_gram(
        1, one,
        lambda: gram_rows(one, [(basis, kept), (field, vecs), (one, vecs)]),
        [(basis, kept), (field, vecs), (one, vecs)])
    packed = share(1, result + pltpu.roll(early, 64, 1))
    low = jnp.concatenate(
        [jnp.zeros((span_one, width), jnp.float32), lanes(packed, 64, span_two),
         jnp.zeros((width - span_two, width), jnp.float32)], axis=0)
    span_gram = span_gram + low + jnp.where(wide_row < wide_lane, low.T, 0.0)
    coef_two_ref[...] = factor(
        lanes(packed, 0, span_two), lanes(packed, span_two, vecs), span_gram, span_two)
    step, body = combine(
        [(image_ref, vecs), (basis, kept), (field, vecs), (one, vecs)], two, None)
    lax.fori_loop(0, chunks, body, 0)


def per_device(
    vectors, basis, potential, hop_table, soc_table, nbr_block, nbr_type, nbr_count, flip_block
):
    blocks, slots = nbr_block.shape
    types, width, _ = hop_table.shape
    vecs, kept = vectors.shape[1], basis.shape[1]
    dom_total = lax.axis_size("dom")
    group_doms = 4 if dom_total % 4 == 0 else 1
    groups = dom_total // group_doms
    block_total = blocks * dom_total
    reach = blocks + 2 * RANGE
    norm = float(2 * blocks * width * dom_total)
    first_block = lax.axis_index("dom") * blocks
    local = jnp.arange(blocks, dtype=jnp.int32)
    offset = (nbr_block - (first_block + local)[:, None] + RANGE) % block_total - RANGE
    place = local[:, None] + offset
    place = jnp.where(
        place < 0, place + blocks + RANGE, jnp.where(place >= blocks, place + RANGE, place))
    live = jnp.arange(slots, dtype=jnp.int32)[None, :] < nbr_count[:, None]
    index = jnp.where(live, nbr_type * reach + place, reach * types)
    index = jnp.concatenate(
        [index, (flip_block - first_block + reach * types + 1)[:, None]], axis=1).reshape(-1)
    cfg = (dom_total, group_doms, blocks, width, types, slots, vecs, kept, norm)
    count = blocks * width
    rows = blocks * vecs
    vmem = pl.BlockSpec(memory_space=pltpu.VMEM)
    f32, bf16 = jnp.float32, jnp.bfloat16
    dma = pltpu.SemaphoreType.DMA
    one, two, coef_one, coef_two = pl.pallas_call(
        functools.partial(kernel, cfg),
        name="krylov",
        out_shape=(
            jax.ShapeDtypeStruct((1, vecs, count), f32),
            jax.ShapeDtypeStruct((1, vecs, count), f32),
            jax.ShapeDtypeStruct((vecs, width), f32),
            jax.ShapeDtypeStruct((vecs, width), f32),
        ),
        in_specs=[vmem] * 5 + [pl.BlockSpec(memory_space=pltpu.SMEM)],
        out_specs=(vmem,) * 4,
        scratch_shapes=[
            pltpu.VMEM((2, rows, width), bf16),
            pltpu.VMEM((2, rows, width), bf16),
            pltpu.VMEM((2, 2 * RANGE * vecs, width), bf16),
            pltpu.VMEM((reach * types + 1 + blocks, vecs, width), f32),
            pltpu.VMEM((vecs, count), f32),
            pltpu.VMEM((kept + 3 * vecs, vecs, width), f32),
            pltpu.VMEM((2, 2 * group_doms, vecs, width), f32),
            pltpu.VMEM((2, groups, vecs, width), f32),
            dma((2, 3)), dma((2, 3)),
            dma((2, 2 * group_doms)), dma((2, 2 * group_doms)),
            dma((2, groups)), dma((2, groups)),
        ],
        compiler_params=pltpu.CompilerParams(
            collective_id=0, has_side_effects=True, vmem_limit_bytes=48 * 1024 * 1024),
    )(vectors, basis, potential, hop_table.reshape(types * width, width), soc_table, index)

    def unpacked(tile, span_count):
        return jnp.concatenate([tile[:, :span_count].T, tile[:, 64:64 + vecs]], axis=0)

    return one, two, unpacked(coef_one, kept + vecs), unpacked(coef_two, kept + 2 * vecs)


def solution(mesh):
    return jax.shard_map(
        per_device,
        mesh=mesh,
        in_specs=(
            P("spin", None, "dom"),
            P("spin", None, "dom"),
            P("spin", "dom"),
            P(),
            P(),
            P("dom", None),
            P("dom", None),
            P("dom"),
            P("dom"),
        ),
        out_specs=(P("spin", None, "dom"), P("spin", None, "dom"), P(), P()),
        check_vma=False,
    )
```

```python
import functools
import jax
import jax.numpy as jnp
from jax import lax
from jax.experimental import pallas as pl
from jax.experimental.pallas import tpu as pltpu
from jax.sharding import PartitionSpec as P

RANGE = 8
MESH = pl.DeviceIdType.MESH
NT = (((1,), (1,)), ((), ()))
NN = (((1,), (0,)), ((), ()))


def high_dot(left, right, dims):
    return lax.dot_general(
        left, right, dims, precision=lax.Precision.HIGHEST, preferred_element_type=jnp.float32
    )


def spread(table, bcast_ref, count, vecs, width):
    for m in range(count):
        bcast_ref[m] = jnp.broadcast_to(table[:, vecs + m:vecs + m + 1], (vecs, width))


def combine(work_ref, bcast_ref, image_row, span_rows, vecs, width, out_ref, ext_out):
    step = 4
    order = [image_row + r for r in range(vecs)] + span_rows

    def cols(tile):
        return pl.ds(pl.multiple_of(tile * width, width), width)

    def body(chunk, carry):
        sums = [None] * step
        for m, r in enumerate(order):
            coef = bcast_ref[m]
            for u in range(step):
                term = coef * work_ref[pl.ds(r, 1), cols(chunk * step + u)]
                sums[u] = term if sums[u] is None else sums[u] + term
        for u in range(step):
            out_ref[:, cols(chunk * step + u)] = sums[u]
        if ext_out is not None:
            for u in range(0, step, 2):
                pair = jnp.concatenate(sums[u:u + 2], axis=0).astype(jnp.bfloat16)
                at = pl.multiple_of((chunk * step + u) * vecs, 2 * vecs)
                ext_out[pl.ds(at, 2 * vecs), :] = pair
        return carry
    return step, body


def kernel(
    cfg,
    vec_hbm, basis_hbm, pot_hbm, hop_hbm, soc_hbm, nbr_hbm, type_hbm, count_hbm, flip_hbm,
    one_hbm, image_hbm, small_ref,
    work_ref, bcast_ref, pot_ref, hop_ref, soc_ref, nbr_ref, type_ref, count_ref, fliploc_ref, table_ref, idx_ref,
    ext_ref, other_ref, halo_ref, prod_ref, stage_a_ref, stage_b_ref,
    load_sem, link_send, link_recv, a_send, a_recv, b_send, b_recv,
):
    dom_total, group_doms, blocks, width, types, slots, vecs, kept, norm = cfg
    span_one = kept + vecs
    span_two = span_one + vecs
    loads = [
        pltpu.make_async_copy(src, dst, load_sem.at[n])
        for n, (src, dst) in enumerate([
            (nbr_hbm, nbr_ref), (type_hbm, type_ref), (count_hbm, count_ref),
            (flip_hbm, fliploc_ref), (vec_hbm.at[0], work_ref.at[pl.ds(kept, vecs)]),
            (basis_hbm.at[0], work_ref.at[pl.ds(0, kept)]), (hop_hbm, hop_ref),
            (pot_hbm, pot_ref), (soc_hbm, soc_ref)])
    ]
    for copy in loads:
        copy.start()
    table_copy = pltpu.make_async_copy(table_ref, idx_ref, load_sem.at[len(loads)])
    groups = dom_total // group_doms
    group_size = 2 * group_doms
    dom, spin = lax.axis_index("dom"), lax.axis_index("spin")
    rank_a = (dom % group_doms) * 2 + spin
    rank_b = dom // group_doms
    dom_base = rank_b * group_doms
    left, right = (dom + dom_total - 1) % dom_total, (dom + 1) % dom_total
    rows = blocks * vecs
    halo_rows = RANGE * vecs
    reach = blocks + 2 * RANGE
    zero_tile = reach * types
    flip_base = zero_tile + 1

    def peer_a(shift):
        other = (rank_a + shift) % group_size
        return (dom_base + other // 2, other % 2)

    def peer_b(shift):
        return (((rank_b + shift) % groups) * group_doms + dom % group_doms, spin)

    barrier = pltpu.get_barrier_semaphore()
    for shift in range(1, group_size):
        pl.semaphore_signal(barrier, inc=1, device_id=peer_a(shift), device_id_type=MESH)
    for shift in range(1, groups):
        pl.semaphore_signal(barrier, inc=1, device_id=peer_b(shift), device_id_type=MESH)
    for side in (left, right):
        pl.semaphore_signal(barrier, inc=1, device_id=(side, spin), device_id_type=MESH)

    lane = lax.broadcasted_iota(jnp.int32, (vecs, width), 1)
    row = lax.broadcasted_iota(jnp.int32, (vecs, width), 0)

    def cols(tile):
        return pl.ds(pl.multiple_of(tile * width, width), width)

    def link_copies(app):
        ext, halo = ext_ref.at[app], halo_ref.at[app]
        tail = pltpu.make_async_remote_copy(
            src_ref=ext.at[pl.ds(rows - halo_rows, halo_rows)],
            dst_ref=halo.at[pl.ds(0, halo_rows)],
            send_sem=link_send.at[app, 0], recv_sem=link_recv.at[app, 0],
            device_id=(right, spin), device_id_type=MESH)
        head = pltpu.make_async_remote_copy(
            src_ref=ext.at[pl.ds(0, halo_rows)],
            dst_ref=halo.at[pl.ds(halo_rows, halo_rows)],
            send_sem=link_send.at[app, 1], recv_sem=link_recv.at[app, 1],
            device_id=(left, spin), device_id_type=MESH)
        flip = pltpu.make_async_remote_copy(
            src_ref=ext, dst_ref=other_ref.at[app],
            send_sem=link_send.at[app, 2], recv_sem=link_recv.at[app, 2],
            device_id=(dom, 1 - spin), device_id_type=MESH)
        return tail, head, flip

    def gram_rows(left_ref, sources):
        count = sum(hi for _, hi in sources)

        def body(tile, sums):
            ours = left_ref[:, cols(tile)]
            picked = [ref[pl.ds(m, 1), cols(tile)] for ref, hi in sources for m in range(hi)]
            return tuple(total + ours * one for total, one in zip(sums, picked))

        sums = lax.fori_loop(
            0, blocks, body, tuple(jnp.zeros((vecs, width), jnp.float32) for _ in range(count)),
            unroll=2)
        out = jnp.zeros((vecs, width), jnp.float32)
        for m, total in enumerate(sums):
            out = jnp.where(lane == m, jnp.sum(total, axis=1, keepdims=True), out)
        return out

    def products(source, count, first):
        def body(pair, carry):
            weights = hop_ref[pl.ds(pl.multiple_of(pair * 2 * width, 2 * width), 2 * width), :]
            out = lax.dot_general(source[...], weights, NT, preferred_element_type=jnp.float32)
            for half in range(2):
                part = out[:, half * width:(half + 1) * width].reshape(count, vecs, width)
                prod_ref[pl.ds((pair * 2 + half) * reach + first, count)] = part
            return carry
        lax.fori_loop(0, types // 2, body, 0)

    def flip_products(app):
        out = lax.dot_general(
            other_ref[app], soc_ref[spin], NT, preferred_element_type=jnp.float32)
        prod_ref[pl.ds(flip_base, blocks)] = out.reshape(blocks, vecs, width)

    def gather(field_ref, low, high):
        def body(block, carry):
            terms = [pot_ref[pl.ds(0, 1), cols(block)] * field_ref[:, cols(block)]]
            for slot in range(slots + 1):
                terms.append(prod_ref[idx_ref[block, slot]])
            while len(terms) > 1:
                terms = [sum(terms[p:p + 2][1:], terms[p]) for p in range(0, len(terms), 2)]
            image_ref[:, cols(block)] = terms[0]
            return carry
        lax.fori_loop(low, high, body, 0, unroll=2)

    def share(app, value):
        def stage(ref, send, recv, rank, size, peer, mine):
            ref[app, rank] = mine
            def copy(shift, slot):
                return pltpu.make_async_remote_copy(
                    src_ref=ref.at[app, rank], dst_ref=ref.at[app, slot],
                    send_sem=send.at[app, shift], recv_sem=recv.at[app, slot],
                    device_id=peer(shift), device_id_type=MESH)
            for shift in range(1, size):
                copy(shift, rank).start()
            for shift in range(1, size):
                copy(shift, (rank + size - shift) % size).wait_recv()
            for shift in range(1, size):
                copy(shift, rank).wait_send()
            total = ref[app, 0]
            for slot in range(1, size):
                total = total + ref[app, slot]
            return total
        value = stage(stage_a_ref, a_send, a_recv, rank_a, group_size, peer_a, value)
        if groups > 1:
            value = stage(stage_b_ref, b_send, b_recv, rank_b, groups, peer_b, value)
        return value * (1.0 / norm)

    def lanes(value, start, count):
        moved = value if start == 0 else pltpu.roll(value, width - start, 1)
        return jnp.where(lane < count, moved, 0.0)

    def tall(pieces):
        pad = width - vecs * len(pieces)
        return jnp.concatenate(list(pieces) + [jnp.zeros((pad, width), jnp.float32)], axis=0)

    def factor(first_t, image_gram, span_gram, span_count):
        total_t = 2.0 * first_t - high_dot(first_t, span_gram, NT)
        moved = high_dot(total_t, span_gram, NT) - first_t
        gram = image_gram + high_dot(moved, tall([total_t]), NT) - high_dot(total_t, tall([first_t]), NT)
        table = jnp.where(lane < vecs, gram, jnp.where(lane == row + vecs, 1.0, 0.0))
        table = table - pltpu.roll(total_t, 2 * vecs, 1)
        lower = jnp.zeros((vecs, width), jnp.float32)
        for j in range(vecs):
            column = jnp.broadcast_to(table[:, j:j + 1], (vecs, width))
            pivot_row = jnp.broadcast_to(table[j:j + 1, :], (vecs, width))
            pivot = jnp.broadcast_to(column[j:j + 1, :], (vecs, width))
            scale = 1.0 / jnp.sqrt(pivot)
            lower = jnp.where((lane == j) & (row >= j), column * scale, lower)
            pivot_row = pivot_row * scale
            table = jnp.where(
                row == j, pivot_row, jnp.where(row > j, table - column * scale * pivot_row, table))
        return total_t + pltpu.roll(lower, span_count, 1), table

    basis = work_ref.at[pl.ds(0, kept)]
    field = work_ref.at[pl.ds(kept, vecs)]
    one = work_ref.at[pl.ds(span_one, vecs)]
    image_ref = work_ref.at[pl.ds(span_two, vecs)]

    for copy in loads[:4]:
        copy.wait()
    local = lax.broadcasted_iota(jnp.int32, (slots, blocks), 1)
    slot_at = lax.broadcasted_iota(jnp.int32, (slots, blocks), 0)
    shift = nbr_ref[...] - (dom * blocks + local) + RANGE
    total = dom_total * blocks
    shift = jnp.where(shift < 0, shift + total, shift)
    shift = jnp.where(shift >= total, shift - total, shift)
    place = local + shift - RANGE
    place = jnp.where(
        place < 0, place + blocks + RANGE, jnp.where(place >= blocks, place + RANGE, place))
    live = slot_at < count_ref[...]
    index = jnp.concatenate([
        jnp.where(live, type_ref[...] * reach + place, zero_tile),
        jnp.broadcast_to(fliploc_ref[...] - dom * blocks + flip_base, (8, blocks)),
        jnp.zeros((width - slots - 8, blocks), jnp.int32)], axis=0)
    table_ref[...] = jnp.clip(index, 0, flip_base + blocks - 1).T
    table_copy.start()
    loads[4].wait()

    def round_body(pair, carry):
        both = jnp.concatenate([field[:, cols(2 * pair)], field[:, cols(2 * pair + 1)]], axis=0)
        ext_ref[0, pl.ds(pl.multiple_of(pair * 2 * vecs, 2 * vecs), 2 * vecs), :] = both.astype(
            jnp.bfloat16)
        return carry

    lax.fori_loop(0, blocks // 2, round_body, 0, unroll=4)
    prod_ref[zero_tile] = jnp.zeros((vecs, width), jnp.float32)
    loads[5].wait()
    low_gram = [gram_rows(basis.at[pl.ds(g * vecs, vecs)], [(basis, (g + 1) * vecs)])
                for g in range(kept // vecs)]
    low_gram.append(gram_rows(field, [(basis, kept), (field, vecs)]))
    for copy in loads[6:] + [table_copy]:
        copy.wait()
    pl.semaphore_wait(barrier, group_size - 1 + groups - 1 + 2)

    def apply_and_gram(app, field_ref, extra, sources):
        tail, head, flip = link_copies(app)
        products(ext_ref.at[app], blocks, 0)
        early = extra()
        flip.wait_recv()
        flip_products(app)
        gather(field_ref, RANGE, blocks - RANGE)
        tail.wait_recv()
        head.wait_recv()
        products(halo_ref.at[app], 2 * RANGE, blocks)
        gather(field_ref, 0, RANGE)
        gather(field_ref, blocks - RANGE, blocks)
        result = gram_rows(image_ref, sources + [(image_ref, vecs)])
        tail.wait_send()
        head.wait_send()
        flip.wait_send()
        return result, early

    for copy in link_copies(0):
        copy.start()
    result, _ = apply_and_gram(0, field, lambda: None, [(basis, kept), (field, vecs)])
    packed = result
    at = span_one + vecs
    for g in range(span_one // vecs):
        packed = packed + pltpu.roll(low_gram[g], at, 1)
        at += (g + 1) * vecs
    packed = share(0, packed)
    pieces = []
    at = span_one + vecs
    for g in range(span_one // vecs):
        pieces.append(lanes(packed, at, (g + 1) * vecs))
        at += (g + 1) * vecs
    low = tall(pieces)
    wide_row = lax.broadcasted_iota(jnp.int32, (width, width), 0) // vecs
    wide_lane = lax.broadcasted_iota(jnp.int32, (width, width), 1) // vecs
    span_gram = low + jnp.where(wide_row < wide_lane, low.T, 0.0)
    coefs, table = factor(
        lanes(packed, 0, span_one), lanes(packed, span_one, vecs), span_gram, span_one)
    small_ref[pl.ds(0, vecs), :] = coefs
    spread(table, bcast_ref, vecs + span_one, vecs, width)

    step, body = combine(
        work_ref, bcast_ref, span_two, list(range(span_one)), vecs, width, one, ext_ref.at[1])
    chunks, edge = blocks // step, RANGE // step
    tail, head, flip = link_copies(1)
    lax.fori_loop(0, edge, body, 0)
    lax.fori_loop(chunks - edge, chunks, body, 0)
    tail.start()
    head.start()
    lax.fori_loop(edge, chunks - edge, body, 0)
    flip.start()
    one_out = pltpu.make_async_copy(
        work_ref.at[pl.ds(span_one, vecs)], one_hbm, load_sem.at[len(loads) + 1])
    one_out.start()

    result, early = apply_and_gram(
        1, one,
        lambda: gram_rows(one, [(basis, kept), (field, vecs), (one, vecs)]),
        [(basis, kept), (field, vecs), (one, vecs)])
    image_out = pltpu.make_async_copy(
        work_ref.at[pl.ds(span_two, vecs)], image_hbm, load_sem.at[len(loads) + 2])
    image_out.start()
    packed = share(1, result + pltpu.roll(early, 64, 1))
    low = jnp.concatenate(
        [jnp.zeros((span_one, width), jnp.float32), lanes(packed, 64, span_two),
         jnp.zeros((width - span_two, width), jnp.float32)], axis=0)
    span_gram = span_gram + low + jnp.where(wide_row < wide_lane, low.T, 0.0)
    coefs, table = factor(
        lanes(packed, 0, span_two), lanes(packed, span_two, vecs), span_gram, span_two)
    small_ref[pl.ds(vecs, vecs), :] = coefs
    small_ref[pl.ds(2 * vecs, vecs), :] = table
    one_out.wait()
    image_out.wait()


def finish(
    cfg, small_ref, vec_hbm, basis_hbm, one_in_hbm, image_hbm,
    one_hbm, two_hbm, coef_one_hbm, coef_two_hbm,
    work_ref, bcast_ref, two_ref, cut_one_ref, cut_two_ref, load_sem, store_sem,
):
    _, _, blocks, width, _, _, vecs, kept, _ = cfg
    span_one = kept + vecs
    span_two = span_one + vecs
    pieces = 4
    step = 4
    chunks = blocks // step // pieces
    span = chunks * step * width
    loads = []
    for piece in range(pieces):
        part = pl.ds(piece * span, span)
        for n, (src, start, count) in enumerate([
            (basis_hbm.at[0], 0, kept), (vec_hbm.at[0], kept, vecs),
            (one_in_hbm, span_one, vecs), (image_hbm, span_two, vecs)]):
            loads.append(pltpu.make_async_copy(
                src.at[:, part], work_ref.at[pl.ds(start, count), part], load_sem.at[piece, n]))
            loads[-1].start()
    cut_one_ref[...] = small_ref[pl.ds(0, vecs), :span_one + vecs]
    cut_two_ref[...] = small_ref[pl.ds(vecs, vecs), :span_two + vecs]
    stores = [
        pltpu.make_async_copy(cut_one_ref, coef_one_hbm, store_sem.at[0]),
        pltpu.make_async_copy(cut_two_ref, coef_two_hbm, store_sem.at[1])]
    for copy in stores:
        copy.start()
    spread(small_ref[pl.ds(2 * vecs, vecs), :], bcast_ref, vecs + span_two, vecs, width)
    step, body = combine(
        work_ref, bcast_ref, span_two, list(range(span_two)), vecs, width, two_ref, None)
    for piece in range(pieces):
        part = pl.ds(piece * span, span)
        for copy in loads[4 * piece:4 * piece + 4]:
            copy.wait()
        stores.append(pltpu.make_async_copy(
            work_ref.at[pl.ds(span_one, vecs), part], one_hbm.at[0, :, part],
            store_sem.at[2 + piece]))
        stores[-1].start()
        lax.fori_loop(piece * chunks, (piece + 1) * chunks, body, 0)
        stores.append(pltpu.make_async_copy(
            two_ref.at[:, part], two_hbm.at[0, :, part], store_sem.at[2 + pieces + piece]))
        stores[-1].start()
    for copy in stores:
        copy.wait()


def per_device(
    vectors, basis, potential, hop_table, soc_table, nbr_block, nbr_type, nbr_count, flip_block
):
    blocks, slots = nbr_block.shape
    types, width, _ = hop_table.shape
    vecs, kept = vectors.shape[1], basis.shape[1]
    dom_total = lax.axis_size("dom")
    group_doms = 4 if dom_total % 4 == 0 else 1
    groups = dom_total // group_doms
    reach = blocks + 2 * RANGE
    norm = float(2 * blocks * width * dom_total)
    cfg = (dom_total, group_doms, blocks, width, types, slots, vecs, kept, norm)
    count = blocks * width
    rows = blocks * vecs
    span_one, span_two = kept + vecs, kept + 2 * vecs
    vmem = pl.BlockSpec(memory_space=pltpu.VMEM)
    hbm = pl.BlockSpec(memory_space=pltpu.HBM)
    f32, bf16, i32 = jnp.float32, jnp.bfloat16, jnp.int32
    dma = pltpu.SemaphoreType.DMA
    shape = jax.ShapeDtypeStruct
    limit = 64 * 1000 * 1000
    one, image, small = pl.pallas_call(
        functools.partial(kernel, cfg),
        name="krylov",
        out_shape=(
            shape((vecs, count), f32),
            shape((vecs, count), f32),
            shape((3 * vecs, width), f32),
        ),
        in_specs=[hbm] * 9,
        out_specs=(hbm, hbm, vmem),
        scratch_shapes=[
            pltpu.VMEM((span_two + vecs, count), f32),
            pltpu.VMEM((span_two + vecs, vecs, width), f32),
            pltpu.VMEM((1, count), f32),
            pltpu.VMEM((types * width, width), bf16),
            pltpu.VMEM(soc_table.shape, bf16),
            pltpu.VMEM((slots, blocks), i32),
            pltpu.VMEM((slots, blocks), i32),
            pltpu.VMEM((1, blocks), i32),
            pltpu.VMEM((1, blocks), i32),
            pltpu.VMEM((blocks, width), i32),
            pltpu.SMEM((blocks, width), i32),
            pltpu.VMEM((2, rows, width), bf16),
            pltpu.VMEM((2, rows, width), bf16),
            pltpu.VMEM((2, 2 * RANGE * vecs, width), bf16),
            pltpu.VMEM((reach * types + 1 + blocks, vecs, width), f32),
            pltpu.VMEM((2, 2 * group_doms, vecs, width), f32),
            pltpu.VMEM((2, groups, vecs, width), f32),
            dma((12,)),
            dma((2, 3)), dma((2, 3)),
            dma((2, 2 * group_doms)), dma((2, 2 * group_doms)),
            dma((2, groups)), dma((2, groups)),
        ],
        compiler_params=pltpu.CompilerParams(
            collective_id=0, has_side_effects=True, vmem_limit_bytes=limit),
    )(
        vectors, basis, potential, hop_table.reshape(types * width, width), soc_table,
        nbr_block.T, nbr_type.T, nbr_count.reshape(1, blocks), flip_block.reshape(1, blocks))
    one, two, coef_one, coef_two = pl.pallas_call(
        functools.partial(finish, cfg),
        name="finish",
        out_shape=(
            shape((1, vecs, count), f32),
            shape((1, vecs, count), f32),
            shape((vecs, span_one + vecs), f32),
            shape((vecs, span_two + vecs), f32),
        ),
        in_specs=[vmem] + [hbm] * 4,
        out_specs=(hbm,) * 4,
        scratch_shapes=[
            pltpu.VMEM((span_two + vecs, count), f32),
            pltpu.VMEM((span_two + vecs, vecs, width), f32),
            pltpu.VMEM((vecs, count), f32),
            pltpu.VMEM((vecs, span_one + vecs), f32),
            pltpu.VMEM((vecs, span_two + vecs), f32),
            dma((4, 4)), dma((10,)),
        ],
        compiler_params=pltpu.CompilerParams(vmem_limit_bytes=limit),
    )(small, vectors, basis, one, image)
    return one, two, coef_one.T, coef_two.T


def solution(mesh):
    return jax.shard_map(
        per_device,
        mesh=mesh,
        in_specs=(
            P("spin", None, "dom"),
            P("spin", None, "dom"),
            P("spin", "dom"),
            P(),
            P(),
            P("dom", None),
            P("dom", None),
            P("dom"),
            P("dom"),
        ),
        out_specs=(P("spin", None, "dom"), P("spin", None, "dom"), P(), P()),
        check_vma=False,
    )
```

```python
import functools
import jax
import jax.numpy as jnp
from jax import lax
from jax.experimental import pallas as pl
from jax.experimental.pallas import tpu as pltpu
from jax.sharding import PartitionSpec as P

RANGE = 8
MESH = pl.DeviceIdType.MESH
NT = (((1,), (1,)), ((), ()))
NN = (((1,), (0,)), ((), ()))


def high_dot(left, right, dims):
    return lax.dot_general(
        left, right, dims, precision=lax.Precision.HIGHEST, preferred_element_type=jnp.float32
    )


def halves(value):
    top = value.astype(jnp.bfloat16)
    return top, (value - top.astype(jnp.float32)).astype(jnp.bfloat16)


def arranged(table, span_count, image_row, vecs, width):
    lane = lax.broadcasted_iota(jnp.int32, (vecs, width), 1)
    spans = jnp.where(lane < span_count, pltpu.roll(table, width - 2 * vecs, 1), 0.0)
    images = (lane >= image_row) & (lane < image_row + vecs)
    return (spans + jnp.where(images, pltpu.roll(table, image_row - vecs, 1), 0.0))[
        :, :image_row + vecs]


def combine(work_ref, coefs, vecs, width, chunk, out_ref, ext_out):
    count = coefs.shape[1]
    ours_top, ours_rest = halves(coefs)

    def dot(left, right):
        return lax.dot_general(left, right, NN, preferred_element_type=jnp.float32)

    def body(piece, carry):
        part = pl.ds(pl.multiple_of(piece * chunk, chunk), chunk)
        top, rest = halves(work_ref[pl.ds(0, count), part])
        out = (dot(ours_top, rest) + dot(ours_rest, top)) + dot(ours_top, top)
        out_ref[:, part] = out
        if ext_out is not None:
            held = chunk // width
            stacked = jnp.concatenate(
                [out[:, u * width:(u + 1) * width] for u in range(held)], axis=0)
            at = pl.multiple_of(piece * held * vecs, held * vecs)
            ext_out[pl.ds(at, held * vecs), :] = stacked.astype(jnp.bfloat16)
        return carry
    return body


def kernel(
    cfg,
    vec_hbm, basis_hbm, pot_hbm, hop_hbm, soc_hbm, nbr_hbm, type_hbm, count_hbm, flip_hbm,
    one_hbm, image_hbm, small_ref,
    work_ref, pot_ref, hop_ref, soc_ref, nbr_ref, type_ref, count_ref, fliploc_ref, table_ref, idx_ref,
    ext_ref, other_ref, halo_ref, prod_ref, stage_a_ref, stage_b_ref,
    load_sem, link_send, link_recv, a_send, a_recv, b_send, b_recv,
):
    dom_total, group_doms, blocks, width, types, slots, vecs, kept, norm = cfg
    span_one = kept + vecs
    span_two = span_one + vecs
    loads = [
        pltpu.make_async_copy(src, dst, load_sem.at[n])
        for n, (src, dst) in enumerate([
            (nbr_hbm, nbr_ref), (type_hbm, type_ref), (count_hbm, count_ref),
            (flip_hbm, fliploc_ref), (vec_hbm.at[0], work_ref.at[pl.ds(kept, vecs)]),
            (basis_hbm.at[0], work_ref.at[pl.ds(0, kept)]), (hop_hbm, hop_ref),
            (pot_hbm, pot_ref), (soc_hbm, soc_ref)])
    ]
    for copy in loads:
        copy.start()
    table_copy = pltpu.make_async_copy(table_ref, idx_ref, load_sem.at[len(loads)])
    groups = dom_total // group_doms
    group_size = 2 * group_doms
    dom, spin = lax.axis_index("dom"), lax.axis_index("spin")
    rank_a = (dom % group_doms) * 2 + spin
    rank_b = dom // group_doms
    dom_base = rank_b * group_doms
    left, right = (dom + dom_total - 1) % dom_total, (dom + 1) % dom_total
    rows = blocks * vecs
    halo_rows = RANGE * vecs
    reach = blocks + 2 * RANGE
    zero_tile = reach * types
    flip_base = zero_tile + 1

    def peer_a(shift):
        other = (rank_a + shift) % group_size
        return (dom_base + other // 2, other % 2)

    def peer_b(shift):
        return (((rank_b + shift) % groups) * group_doms + dom % group_doms, spin)

    barrier = pltpu.get_barrier_semaphore()
    for shift in range(1, group_size):
        pl.semaphore_signal(barrier, inc=1, device_id=peer_a(shift), device_id_type=MESH)
    for shift in range(1, groups):
        pl.semaphore_signal(barrier, inc=1, device_id=peer_b(shift), device_id_type=MESH)
    for side in (left, right):
        pl.semaphore_signal(barrier, inc=1, device_id=(side, spin), device_id_type=MESH)

    lane = lax.broadcasted_iota(jnp.int32, (vecs, width), 1)
    row = lax.broadcasted_iota(jnp.int32, (vecs, width), 0)

    def cols(tile):
        return pl.ds(pl.multiple_of(tile * width, width), width)

    def link_copies(app):
        ext, halo = ext_ref.at[app], halo_ref.at[app]
        tail = pltpu.make_async_remote_copy(
            src_ref=ext.at[pl.ds(rows - halo_rows, halo_rows)],
            dst_ref=halo.at[pl.ds(0, halo_rows)],
            send_sem=link_send.at[app, 0], recv_sem=link_recv.at[app, 0],
            device_id=(right, spin), device_id_type=MESH)
        head = pltpu.make_async_remote_copy(
            src_ref=ext.at[pl.ds(0, halo_rows)],
            dst_ref=halo.at[pl.ds(halo_rows, halo_rows)],
            send_sem=link_send.at[app, 1], recv_sem=link_recv.at[app, 1],
            device_id=(left, spin), device_id_type=MESH)
        flip = pltpu.make_async_remote_copy(
            src_ref=ext, dst_ref=other_ref.at[app],
            send_sem=link_send.at[app, 2], recv_sem=link_recv.at[app, 2],
            device_id=(dom, 1 - spin), device_id_type=MESH)
        return tail, head, flip

    def gram_rows(start, rows, count):
        chunk = 2048

        def dot(left, right):
            return lax.dot_general(left, right, NT, preferred_element_type=jnp.float32)

        def body(piece, total):
            part = pl.ds(pl.multiple_of(piece * chunk, chunk), chunk)
            ours_top, ours_rest = halves(work_ref[pl.ds(start, rows), part])
            top, rest = halves(work_ref[pl.ds(0, count), part])
            return total + (dot(ours_top, rest) + dot(ours_rest, top)) + dot(ours_top, top)

        out = lax.fori_loop(
            0, blocks * width // chunk, body, jnp.zeros((rows, count), jnp.float32))
        return jnp.concatenate([out, jnp.zeros((rows, width - count), jnp.float32)], axis=1)

    def products(source, count, first):
        def body(pair, carry):
            weights = hop_ref[pl.ds(pl.multiple_of(pair * 2 * width, 2 * width), 2 * width), :]
            out = lax.dot_general(source[...], weights, NT, preferred_element_type=jnp.float32)
            for half in range(2):
                part = out[:, half * width:(half + 1) * width].reshape(count, vecs, width)
                prod_ref[pl.ds((pair * 2 + half) * reach + first, count)] = part
            return carry
        lax.fori_loop(0, types // 2, body, 0)

    def flip_products(app):
        out = lax.dot_general(
            other_ref[app], soc_ref[spin], NT, preferred_element_type=jnp.float32)
        prod_ref[pl.ds(flip_base, blocks)] = out.reshape(blocks, vecs, width)

    def gather(field_ref, low, high):
        def body(block, carry):
            terms = [pot_ref[pl.ds(0, 1), cols(block)] * field_ref[:, cols(block)]]
            for slot in range(slots + 1):
                terms.append(prod_ref[idx_ref[block, slot]])
            while len(terms) > 1:
                terms = [sum(terms[p:p + 2][1:], terms[p]) for p in range(0, len(terms), 2)]
            image_ref[:, cols(block)] = terms[0]
            return carry
        lax.fori_loop(low, high, body, 0, unroll=2)

    def share(app, value):
        def stage(ref, send, recv, rank, size, peer, mine):
            ref[app, rank] = mine
            def copy(shift, slot):
                return pltpu.make_async_remote_copy(
                    src_ref=ref.at[app, rank], dst_ref=ref.at[app, slot],
                    send_sem=send.at[app, shift], recv_sem=recv.at[app, slot],
                    device_id=peer(shift), device_id_type=MESH)
            for shift in range(1, size):
                copy(shift, rank).start()
            for shift in range(1, size):
                copy(shift, (rank + size - shift) % size).wait_recv()
            for shift in range(1, size):
                copy(shift, rank).wait_send()
            total = ref[app, 0]
            for slot in range(1, size):
                total = total + ref[app, slot]
            return total
        value = stage(stage_a_ref, a_send, a_recv, rank_a, group_size, peer_a, value)
        if groups > 1:
            value = stage(stage_b_ref, b_send, b_recv, rank_b, groups, peer_b, value)
        return value * (1.0 / norm)

    def lanes(value, start, count):
        moved = value if start == 0 else pltpu.roll(value, width - start, 1)
        return jnp.where(lane < count, moved, 0.0)

    def tall(pieces):
        pad = width - vecs * len(pieces)
        return jnp.concatenate(list(pieces) + [jnp.zeros((pad, width), jnp.float32)], axis=0)

    def factor(first_t, image_gram, span_gram, span_count):
        total_t = 2.0 * first_t - high_dot(first_t, span_gram, NT)
        moved = high_dot(total_t, span_gram, NT) - first_t
        gram = image_gram + high_dot(moved, tall([total_t]), NT) - high_dot(total_t, tall([first_t]), NT)
        table = jnp.where(lane < vecs, gram, jnp.where(lane == row + vecs, 1.0, 0.0))
        table = table - pltpu.roll(total_t, 2 * vecs, 1)
        lower = jnp.zeros((vecs, width), jnp.float32)
        for j in range(vecs):
            column = jnp.broadcast_to(table[:, j:j + 1], (vecs, width))
            pivot_row = jnp.broadcast_to(table[j:j + 1, :], (vecs, width))
            pivot = jnp.broadcast_to(column[j:j + 1, :], (vecs, width))
            scale = 1.0 / jnp.sqrt(pivot)
            lower = jnp.where((lane == j) & (row >= j), column * scale, lower)
            pivot_row = pivot_row * scale
            table = jnp.where(
                row == j, pivot_row, jnp.where(row > j, table - column * scale * pivot_row, table))
        return total_t + pltpu.roll(lower, span_count, 1), table

    basis = work_ref.at[pl.ds(0, kept)]
    field = work_ref.at[pl.ds(kept, vecs)]
    one = work_ref.at[pl.ds(span_one, vecs)]
    image_ref = work_ref.at[pl.ds(span_two, vecs)]

    for copy in loads[:4]:
        copy.wait()
    local = lax.broadcasted_iota(jnp.int32, (slots, blocks), 1)
    slot_at = lax.broadcasted_iota(jnp.int32, (slots, blocks), 0)
    shift = nbr_ref[...] - (dom * blocks + local) + RANGE
    total = dom_total * blocks
    shift = jnp.where(shift < 0, shift + total, shift)
    shift = jnp.where(shift >= total, shift - total, shift)
    place = local + shift - RANGE
    place = jnp.where(
        place < 0, place + blocks + RANGE, jnp.where(place >= blocks, place + RANGE, place))
    live = slot_at < count_ref[...]
    index = jnp.concatenate([
        jnp.where(live, type_ref[...] * reach + place, zero_tile),
        jnp.broadcast_to(fliploc_ref[...] - dom * blocks + flip_base, (8, blocks)),
        jnp.zeros((width - slots - 8, blocks), jnp.int32)], axis=0)
    table_ref[...] = jnp.clip(index, 0, flip_base + blocks - 1).T
    table_copy.start()
    one[...] = jnp.zeros(one.shape, jnp.float32)
    loads[4].wait()

    def round_body(pair, carry):
        both = jnp.concatenate([field[:, cols(2 * pair)], field[:, cols(2 * pair + 1)]], axis=0)
        ext_ref[0, pl.ds(pl.multiple_of(pair * 2 * vecs, 2 * vecs), 2 * vecs), :] = both.astype(
            jnp.bfloat16)
        return carry

    lax.fori_loop(0, blocks // 2, round_body, 0, unroll=4)
    prod_ref[zero_tile] = jnp.zeros((vecs, width), jnp.float32)
    loads[5].wait()
    whole = gram_rows(0, span_one, span_one)
    low_gram = [jnp.where(lane < (g + 1) * vecs, whole[g * vecs:(g + 1) * vecs, :], 0.0)
                for g in range(span_one // vecs)]
    for copy in loads[6:] + [table_copy]:
        copy.wait()
    pl.semaphore_wait(barrier, group_size - 1 + groups - 1 + 2)

    def apply_and_gram(app, field_ref, extra):
        tail, head, flip = link_copies(app)
        products(ext_ref.at[app], blocks, 0)
        early = extra()
        flip.wait_recv()
        flip_products(app)
        gather(field_ref, RANGE, blocks - RANGE)
        tail.wait_recv()
        head.wait_recv()
        products(halo_ref.at[app], 2 * RANGE, blocks)
        gather(field_ref, 0, RANGE)
        gather(field_ref, blocks - RANGE, blocks)
        result = gram_rows(span_two, vecs, span_two + vecs)
        tail.wait_send()
        head.wait_send()
        flip.wait_send()
        return result, early

    for copy in link_copies(0):
        copy.start()
    result, _ = apply_and_gram(0, field, lambda: None)
    result = jnp.where(lane < span_one, result, jnp.where(
        lane < span_two, pltpu.roll(result, width - vecs, 1), 0.0))
    packed = result
    at = span_one + vecs
    for g in range(span_one // vecs):
        packed = packed + pltpu.roll(low_gram[g], at, 1)
        at += (g + 1) * vecs
    packed = share(0, packed)
    pieces = []
    at = span_one + vecs
    for g in range(span_one // vecs):
        pieces.append(lanes(packed, at, (g + 1) * vecs))
        at += (g + 1) * vecs
    low = tall(pieces)
    wide_row = lax.broadcasted_iota(jnp.int32, (width, width), 0) // vecs
    wide_lane = lax.broadcasted_iota(jnp.int32, (width, width), 1) // vecs
    span_gram = low + jnp.where(wide_row < wide_lane, low.T, 0.0)
    coefs, table = factor(
        lanes(packed, 0, span_one), lanes(packed, span_one, vecs), span_gram, span_one)
    small_ref[pl.ds(0, vecs), :] = coefs
    chunk = RANGE * width
    body = combine(
        work_ref, arranged(table, span_one, span_two, vecs, width), vecs, width, chunk, one,
        ext_ref.at[1])
    chunks, edge = blocks // RANGE, 1
    tail, head, flip = link_copies(1)
    lax.fori_loop(0, edge, body, 0)
    lax.fori_loop(chunks - edge, chunks, body, 0)
    tail.start()
    head.start()
    lax.fori_loop(edge, chunks - edge, body, 0)
    flip.start()
    one_out = pltpu.make_async_copy(
        work_ref.at[pl.ds(span_one, vecs)], one_hbm, load_sem.at[len(loads) + 1])
    one_out.start()

    result, early = apply_and_gram(
        1, one,
        lambda: gram_rows(span_one, vecs, span_two))
    image_out = pltpu.make_async_copy(
        work_ref.at[pl.ds(span_two, vecs)], image_hbm, load_sem.at[len(loads) + 2])
    image_out.start()
    packed = share(1, result + pltpu.roll(early, 64, 1))
    low = jnp.concatenate(
        [jnp.zeros((span_one, width), jnp.float32), lanes(packed, 64, span_two),
         jnp.zeros((width - span_two, width), jnp.float32)], axis=0)
    span_gram = span_gram + low + jnp.where(wide_row < wide_lane, low.T, 0.0)
    coefs, table = factor(
        lanes(packed, 0, span_two), lanes(packed, span_two, vecs), span_gram, span_two)
    small_ref[pl.ds(vecs, vecs), :] = coefs
    small_ref[pl.ds(2 * vecs, vecs), :] = table
    one_out.wait()
    image_out.wait()


def finish(
    cfg, small_ref, vec_hbm, basis_hbm, one_in_hbm, image_hbm,
    one_hbm, two_hbm, coef_one_hbm, coef_two_hbm,
    work_ref, two_ref, cut_one_ref, cut_two_ref, load_sem, store_sem,
):
    _, _, blocks, width, _, _, vecs, kept, _ = cfg
    span_one = kept + vecs
    span_two = span_one + vecs
    pieces = 4
    chunk = RANGE * width
    chunks = blocks // RANGE // pieces
    span = chunks * chunk
    loads = []
    for piece in range(pieces):
        part = pl.ds(piece * span, span)
        for n, (src, start, count) in enumerate([
            (basis_hbm.at[0], 0, kept), (vec_hbm.at[0], kept, vecs),
            (one_in_hbm, span_one, vecs), (image_hbm, span_two, vecs)]):
            loads.append(pltpu.make_async_copy(
                src.at[:, part], work_ref.at[pl.ds(start, count), part], load_sem.at[piece, n]))
            loads[-1].start()
    cut_one_ref[...] = small_ref[pl.ds(0, vecs), :span_one + vecs]
    cut_two_ref[...] = small_ref[pl.ds(vecs, vecs), :span_two + vecs]
    stores = [
        pltpu.make_async_copy(cut_one_ref, coef_one_hbm, store_sem.at[0]),
        pltpu.make_async_copy(cut_two_ref, coef_two_hbm, store_sem.at[1])]
    for copy in stores:
        copy.start()
    body = combine(
        work_ref,
        arranged(small_ref[pl.ds(2 * vecs, vecs), :], span_two, span_two, vecs, width),
        vecs, width, chunk, two_ref, None)
    for piece in range(pieces):
        part = pl.ds(piece * span, span)
        for copy in loads[4 * piece:4 * piece + 4]:
            copy.wait()
        stores.append(pltpu.make_async_copy(
            work_ref.at[pl.ds(span_one, vecs), part], one_hbm.at[0, :, part],
            store_sem.at[2 + piece]))
        stores[-1].start()
        lax.fori_loop(piece * chunks, (piece + 1) * chunks, body, 0)
        stores.append(pltpu.make_async_copy(
            two_ref.at[:, part], two_hbm.at[0, :, part], store_sem.at[2 + pieces + piece]))
        stores[-1].start()
    for copy in stores:
        copy.wait()


def per_device(
    vectors, basis, potential, hop_table, soc_table, nbr_block, nbr_type, nbr_count, flip_block
):
    blocks, slots = nbr_block.shape
    types, width, _ = hop_table.shape
    vecs, kept = vectors.shape[1], basis.shape[1]
    dom_total = lax.axis_size("dom")
    group_doms = 4 if dom_total % 4 == 0 else 1
    groups = dom_total // group_doms
    reach = blocks + 2 * RANGE
    norm = float(2 * blocks * width * dom_total)
    cfg = (dom_total, group_doms, blocks, width, types, slots, vecs, kept, norm)
    count = blocks * width
    rows = blocks * vecs
    span_one, span_two = kept + vecs, kept + 2 * vecs
    vmem = pl.BlockSpec(memory_space=pltpu.VMEM)
    hbm = pl.BlockSpec(memory_space=pltpu.HBM)
    f32, bf16, i32 = jnp.float32, jnp.bfloat16, jnp.int32
    dma = pltpu.SemaphoreType.DMA
    shape = jax.ShapeDtypeStruct
    limit = 64 * 1000 * 1000
    one, image, small = pl.pallas_call(
        functools.partial(kernel, cfg),
        name="krylov",
        out_shape=(
            shape((vecs, count), f32),
            shape((vecs, count), f32),
            shape((3 * vecs, width), f32),
        ),
        in_specs=[hbm] * 9,
        out_specs=(hbm, hbm, vmem),
        scratch_shapes=[
            pltpu.VMEM((span_two + vecs, count), f32),
            pltpu.VMEM((1, count), f32),
            pltpu.VMEM((types * width, width), bf16),
            pltpu.VMEM(soc_table.shape, bf16),
            pltpu.VMEM((slots, blocks), i32),
            pltpu.VMEM((slots, blocks), i32),
            pltpu.VMEM((1, blocks), i32),
            pltpu.VMEM((1, blocks), i32),
            pltpu.VMEM((blocks, width), i32),
            pltpu.SMEM((blocks, width), i32),
            pltpu.VMEM((2, rows, width), bf16),
            pltpu.VMEM((2, rows, width), bf16),
            pltpu.VMEM((2, 2 * RANGE * vecs, width), bf16),
            pltpu.VMEM((reach * types + 1 + blocks, vecs, width), f32),
            pltpu.VMEM((2, 2 * group_doms, vecs, width), f32),
            pltpu.VMEM((2, groups, vecs, width), f32),
            dma((12,)),
            dma((2, 3)), dma((2, 3)),
            dma((2, 2 * group_doms)), dma((2, 2 * group_doms)),
            dma((2, groups)), dma((2, groups)),
        ],
        compiler_params=pltpu.CompilerParams(
            collective_id=0, has_side_effects=True, vmem_limit_bytes=limit),
    )(
        vectors, basis, potential, hop_table.reshape(types * width, width), soc_table,
        nbr_block.T, nbr_type.T, nbr_count.reshape(1, blocks), flip_block.reshape(1, blocks))
    one, two, coef_one, coef_two = pl.pallas_call(
        functools.partial(finish, cfg),
        name="finish",
        out_shape=(
            shape((1, vecs, count), f32),
            shape((1, vecs, count), f32),
            shape((vecs, span_one + vecs), f32),
            shape((vecs, span_two + vecs), f32),
        ),
        in_specs=[vmem] + [hbm] * 4,
        out_specs=(hbm,) * 4,
        scratch_shapes=[
            pltpu.VMEM((span_two + vecs, count), f32),
            pltpu.VMEM((vecs, count), f32),
            pltpu.VMEM((vecs, span_one + vecs), f32),
            pltpu.VMEM((vecs, span_two + vecs), f32),
            dma((4, 4)), dma((10,)),
        ],
        compiler_params=pltpu.CompilerParams(vmem_limit_bytes=limit),
    )(small, vectors, basis, one, image)
    return one, two, coef_one.T, coef_two.T


def solution(mesh):
    return jax.shard_map(
        per_device,
        mesh=mesh,
        in_specs=(
            P("spin", None, "dom"),
            P("spin", None, "dom"),
            P("spin", "dom"),
            P(),
            P(),
            P("dom", None),
            P("dom", None),
            P("dom"),
            P("dom"),
        ),
        out_specs=(P("spin", None, "dom"), P("spin", None, "dom"), P(), P()),
        check_vma=False,
    )
```

```python
import functools
import jax
import jax.numpy as jnp
from jax import lax
from jax.experimental import pallas as pl
from jax.experimental.pallas import tpu as pltpu
from jax.sharding import PartitionSpec as P

RANGE = 8
MESH = pl.DeviceIdType.MESH
NT = (((1,), (1,)), ((), ()))
NN = (((1,), (0,)), ((), ()))


def high_dot(left, right, dims):
    return lax.dot_general(
        left, right, dims, precision=lax.Precision.HIGHEST, preferred_element_type=jnp.float32
    )


def spread(table, bcast_ref, count, vecs, width):
    for m in range(count):
        bcast_ref[m] = jnp.broadcast_to(table[:, vecs + m:vecs + m + 1], (vecs, width))


def combine(work_ref, bcast_ref, image_row, span_rows, vecs, width, out_ref, ext_out):
    step = 4
    order = [image_row + r for r in range(vecs)] + span_rows

    def cols(tile):
        return pl.ds(pl.multiple_of(tile * width, width), width)

    def body(chunk, carry):
        sums = [None] * step
        for m, r in enumerate(order):
            coef = bcast_ref[m]
            for u in range(step):
                term = coef * work_ref[pl.ds(r, 1), cols(chunk * step + u)]
                sums[u] = term if sums[u] is None else sums[u] + term
        for u in range(step):
            out_ref[:, cols(chunk * step + u)] = sums[u]
        if ext_out is not None:
            for u in range(0, step, 2):
                pair = jnp.concatenate(sums[u:u + 2], axis=0).astype(jnp.bfloat16)
                at = pl.multiple_of((chunk * step + u) * vecs, 2 * vecs)
                ext_out[pl.ds(at, 2 * vecs), :] = pair
        return carry
    return step, body


def kernel(
    cfg,
    vec_hbm, basis_hbm, pot_hbm, hop_hbm, soc_hbm, nbr_hbm, type_hbm, count_hbm, flip_hbm,
    one_hbm, image_hbm, small_ref,
    work_ref, bcast_ref, pot_ref, hop_ref, soc_ref, nbr_ref, type_ref, count_ref, fliploc_ref, table_ref, idx_ref,
    ext_ref, other_ref, halo_ref, prod_ref, stage_a_ref, stage_b_ref,
    load_sem, link_send, link_recv, a_send, a_recv, b_send, b_recv,
):
    dom_total, group_doms, blocks, width, types, slots, vecs, kept, norm = cfg
    span_one = kept + vecs
    span_two = span_one + vecs
    loads = [
        pltpu.make_async_copy(src, dst, load_sem.at[n])
        for n, (src, dst) in enumerate([
            (nbr_hbm, nbr_ref), (type_hbm, type_ref), (count_hbm, count_ref),
            (flip_hbm, fliploc_ref), (vec_hbm.at[0], work_ref.at[pl.ds(kept, vecs)]),
            (basis_hbm.at[0], work_ref.at[pl.ds(0, kept)]), (hop_hbm, hop_ref),
            (pot_hbm, pot_ref), (soc_hbm, soc_ref)])
    ]
    for copy in loads:
        copy.start()
    table_copy = pltpu.make_async_copy(table_ref, idx_ref, load_sem.at[len(loads)])
    groups = dom_total // group_doms
    group_size = 2 * group_doms
    dom, spin = lax.axis_index("dom"), lax.axis_index("spin")
    rank_a = (dom % group_doms) * 2 + spin
    rank_b = dom // group_doms
    dom_base = rank_b * group_doms
    left, right = (dom + dom_total - 1) % dom_total, (dom + 1) % dom_total
    rows = blocks * vecs
    halo_rows = RANGE * vecs
    reach = blocks + 2 * RANGE
    zero_tile = reach * types
    flip_base = zero_tile + 1

    def peer_a(shift):
        other = (rank_a + shift) % group_size
        return (dom_base + other // 2, other % 2)

    def peer_b(shift):
        return (((rank_b + shift) % groups) * group_doms + dom % group_doms, spin)

    barrier = pltpu.get_barrier_semaphore()
    for shift in range(1, group_size):
        pl.semaphore_signal(barrier, inc=1, device_id=peer_a(shift), device_id_type=MESH)
    for shift in range(1, groups):
        pl.semaphore_signal(barrier, inc=1, device_id=peer_b(shift), device_id_type=MESH)
    for side in (left, right):
        pl.semaphore_signal(barrier, inc=1, device_id=(side, spin), device_id_type=MESH)

    lane = lax.broadcasted_iota(jnp.int32, (vecs, width), 1)
    row = lax.broadcasted_iota(jnp.int32, (vecs, width), 0)

    def cols(tile):
        return pl.ds(pl.multiple_of(tile * width, width), width)

    def link_copies(app):
        ext, halo = ext_ref.at[app], halo_ref.at[app]
        tail = pltpu.make_async_remote_copy(
            src_ref=ext.at[pl.ds(rows - halo_rows, halo_rows)],
            dst_ref=halo.at[pl.ds(0, halo_rows)],
            send_sem=link_send.at[app, 0], recv_sem=link_recv.at[app, 0],
            device_id=(right, spin), device_id_type=MESH)
        head = pltpu.make_async_remote_copy(
            src_ref=ext.at[pl.ds(0, halo_rows)],
            dst_ref=halo.at[pl.ds(halo_rows, halo_rows)],
            send_sem=link_send.at[app, 1], recv_sem=link_recv.at[app, 1],
            device_id=(left, spin), device_id_type=MESH)
        flip = pltpu.make_async_remote_copy(
            src_ref=ext, dst_ref=other_ref.at[app],
            send_sem=link_send.at[app, 2], recv_sem=link_recv.at[app, 2],
            device_id=(dom, 1 - spin), device_id_type=MESH)
        return tail, head, flip

    def gram_rows(left_ref, sources):
        count = sum(hi for _, hi in sources)

        def body(tile, sums):
            ours = left_ref[:, cols(tile)]
            picked = [ref[pl.ds(m, 1), cols(tile)] for ref, hi in sources for m in range(hi)]
            return tuple(total + ours * one for total, one in zip(sums, picked))

        sums = lax.fori_loop(
            0, blocks, body, tuple(jnp.zeros((vecs, width), jnp.float32) for _ in range(count)),
            unroll=2)
        out = jnp.zeros((vecs, width), jnp.float32)
        for m, total in enumerate(sums):
            out = jnp.where(lane == m, jnp.sum(total, axis=1, keepdims=True), out)
        return out

    def products(source, count, first):
        def body(pair, carry):
            weights = hop_ref[pl.ds(pl.multiple_of(pair * 2 * width, 2 * width), 2 * width), :]
            out = lax.dot_general(source[...], weights, NT, preferred_element_type=jnp.float32)
            for half in range(2):
                part = out[:, half * width:(half + 1) * width].reshape(count, vecs, width)
                prod_ref[pl.ds((pair * 2 + half) * reach + first, count)] = part
            return carry
        lax.fori_loop(0, types // 2, body, 0)

    def flip_products(app):
        out = lax.dot_general(
            other_ref[app], soc_ref[spin], NT, preferred_element_type=jnp.float32)
        prod_ref[pl.ds(flip_base, blocks)] = out.reshape(blocks, vecs, width)

    def gather(field_ref, low, high):
        def body(block, carry):
            terms = [pot_ref[pl.ds(0, 1), cols(block)] * field_ref[:, cols(block)]]
            for slot in range(slots + 1):
                terms.append(prod_ref[idx_ref[block, slot]])
            while len(terms) > 1:
                terms = [sum(terms[p:p + 2][1:], terms[p]) for p in range(0, len(terms), 2)]
            image_ref[:, cols(block)] = terms[0]
            return carry
        lax.fori_loop(low, high, body, 0, unroll=2)

    def share(app, value):
        def stage(ref, send, recv, rank, size, peer, mine):
            ref[app, rank] = mine
            def copy(shift, slot):
                return pltpu.make_async_remote_copy(
                    src_ref=ref.at[app, rank], dst_ref=ref.at[app, slot],
                    send_sem=send.at[app, shift], recv_sem=recv.at[app, slot],
                    device_id=peer(shift), device_id_type=MESH)
            for shift in range(1, size):
                copy(shift, rank).start()
            for shift in range(1, size):
                copy(shift, (rank + size - shift) % size).wait_recv()
            for shift in range(1, size):
                copy(shift, rank).wait_send()
            total = ref[app, 0]
            for slot in range(1, size):
                total = total + ref[app, slot]
            return total
        value = stage(stage_a_ref, a_send, a_recv, rank_a, group_size, peer_a, value)
        if groups > 1:
            value = stage(stage_b_ref, b_send, b_recv, rank_b, groups, peer_b, value)
        return value * (1.0 / norm)

    def lanes(value, start, count):
        moved = value if start == 0 else pltpu.roll(value, width - start, 1)
        return jnp.where(lane < count, moved, 0.0)

    def tall(pieces):
        pad = width - vecs * len(pieces)
        return jnp.concatenate(list(pieces) + [jnp.zeros((pad, width), jnp.float32)], axis=0)

    def factor(first_t, image_gram, span_gram, span_count):
        total_t = 2.0 * first_t - high_dot(first_t, span_gram, NT)
        moved = high_dot(total_t, span_gram, NT) - first_t
        gram = image_gram + high_dot(moved, tall([total_t]), NT) - high_dot(total_t, tall([first_t]), NT)
        table = jnp.where(lane < vecs, gram, jnp.where(lane == row + vecs, 1.0, 0.0))
        table = table - pltpu.roll(total_t, 2 * vecs, 1)
        lower = jnp.zeros((vecs, width), jnp.float32)
        for j in range(vecs):
            column = jnp.broadcast_to(table[:, j:j + 1], (vecs, width))
            pivot_row = jnp.broadcast_to(table[j:j + 1, :], (vecs, width))
            pivot = jnp.broadcast_to(column[j:j + 1, :], (vecs, width))
            scale = 1.0 / jnp.sqrt(pivot)
            lower = jnp.where((lane == j) & (row >= j), column * scale, lower)
            pivot_row = pivot_row * scale
            table = jnp.where(
                row == j, pivot_row, jnp.where(row > j, table - column * scale * pivot_row, table))
        return total_t + pltpu.roll(lower, span_count, 1), table

    basis = work_ref.at[pl.ds(0, kept)]
    field = work_ref.at[pl.ds(kept, vecs)]
    one = work_ref.at[pl.ds(span_one, vecs)]
    image_ref = work_ref.at[pl.ds(span_two, vecs)]

    for copy in loads[:4]:
        copy.wait()
    local = lax.broadcasted_iota(jnp.int32, (slots, blocks), 1)
    slot_at = lax.broadcasted_iota(jnp.int32, (slots, blocks), 0)
    shift = nbr_ref[...] - (dom * blocks + local) + RANGE
    total = dom_total * blocks
    shift = jnp.where(shift < 0, shift + total, shift)
    shift = jnp.where(shift >= total, shift - total, shift)
    place = local + shift - RANGE
    place = jnp.where(
        place < 0, place + blocks + RANGE, jnp.where(place >= blocks, place + RANGE, place))
    live = slot_at < count_ref[...]
    index = jnp.concatenate([
        jnp.where(live, type_ref[...] * reach + place, zero_tile),
        jnp.broadcast_to(fliploc_ref[...] - dom * blocks + flip_base, (8, blocks)),
        jnp.zeros((width - slots - 8, blocks), jnp.int32)], axis=0)
    table_ref[...] = jnp.clip(index, 0, flip_base + blocks - 1).T
    table_copy.start()
    loads[4].wait()

    def round_body(pair, carry):
        both = jnp.concatenate([field[:, cols(2 * pair)], field[:, cols(2 * pair + 1)]], axis=0)
        ext_ref[0, pl.ds(pl.multiple_of(pair * 2 * vecs, 2 * vecs), 2 * vecs), :] = both.astype(
            jnp.bfloat16)
        return carry

    lax.fori_loop(0, blocks // 2, round_body, 0, unroll=4)
    prod_ref[zero_tile] = jnp.zeros((vecs, width), jnp.float32)
    pl.semaphore_wait(barrier, group_size - 1 + groups - 1 + 2)
    for copy in link_copies(0):
        copy.start()
    loads[5].wait()
    low_gram = [gram_rows(basis.at[pl.ds(g * vecs, vecs)], [(basis, (g + 1) * vecs)])
                for g in range(kept // vecs)]
    low_gram.append(gram_rows(field, [(basis, kept), (field, vecs)]))
    for copy in loads[6:] + [table_copy]:
        copy.wait()

    def apply_and_gram(app, field_ref, extra, sources):
        tail, head, flip = link_copies(app)
        products(ext_ref.at[app], blocks, 0)
        early = extra()
        flip.wait_recv()
        flip_products(app)
        gather(field_ref, RANGE, blocks - RANGE)
        tail.wait_recv()
        head.wait_recv()
        products(halo_ref.at[app], 2 * RANGE, blocks)
        gather(field_ref, 0, RANGE)
        gather(field_ref, blocks - RANGE, blocks)
        result = gram_rows(image_ref, sources + [(image_ref, vecs)])
        tail.wait_send()
        head.wait_send()
        flip.wait_send()
        return result, early

    result, _ = apply_and_gram(0, field, lambda: None, [(basis, kept), (field, vecs)])
    packed = result
    at = span_one + vecs
    for g in range(span_one // vecs):
        packed = packed + pltpu.roll(low_gram[g], at, 1)
        at += (g + 1) * vecs
    packed = share(0, packed)
    pieces = []
    at = span_one + vecs
    for g in range(span_one // vecs):
        pieces.append(lanes(packed, at, (g + 1) * vecs))
        at += (g + 1) * vecs
    low = tall(pieces)
    wide_row = lax.broadcasted_iota(jnp.int32, (width, width), 0) // vecs
    wide_lane = lax.broadcasted_iota(jnp.int32, (width, width), 1) // vecs
    span_gram = low + jnp.where(wide_row < wide_lane, low.T, 0.0)
    coefs, table = factor(
        lanes(packed, 0, span_one), lanes(packed, span_one, vecs), span_gram, span_one)
    small_ref[pl.ds(0, vecs), :] = coefs
    spread(table, bcast_ref, vecs + span_one, vecs, width)

    step, body = combine(
        work_ref, bcast_ref, span_two, list(range(span_one)), vecs, width, one, ext_ref.at[1])
    chunks, edge = blocks // step, RANGE // step
    tail, head, flip = link_copies(1)
    lax.fori_loop(0, edge, body, 0)
    lax.fori_loop(chunks - edge, chunks, body, 0)
    tail.start()
    head.start()
    lax.fori_loop(edge, chunks - edge, body, 0)
    flip.start()
    one_out = pltpu.make_async_copy(
        work_ref.at[pl.ds(span_one, vecs)], one_hbm, load_sem.at[len(loads) + 1])
    one_out.start()

    result, early = apply_and_gram(
        1, one,
        lambda: gram_rows(one, [(basis, kept), (field, vecs), (one, vecs)]),
        [(basis, kept), (field, vecs), (one, vecs)])
    image_out = pltpu.make_async_copy(
        work_ref.at[pl.ds(span_two, vecs)], image_hbm, load_sem.at[len(loads) + 2])
    image_out.start()
    packed = share(1, result + pltpu.roll(early, 64, 1))
    low = jnp.concatenate(
        [jnp.zeros((span_one, width), jnp.float32), lanes(packed, 64, span_two),
         jnp.zeros((width - span_two, width), jnp.float32)], axis=0)
    span_gram = span_gram + low + jnp.where(wide_row < wide_lane, low.T, 0.0)
    coefs, table = factor(
        lanes(packed, 0, span_two), lanes(packed, span_two, vecs), span_gram, span_two)
    small_ref[pl.ds(vecs, vecs), :] = coefs
    small_ref[pl.ds(2 * vecs, vecs), :] = table
    one_out.wait()
    image_out.wait()


def finish(
    cfg, small_ref, vec_hbm, basis_hbm, one_in_hbm, image_hbm,
    one_hbm, two_hbm, coef_one_hbm, coef_two_hbm,
    work_ref, bcast_ref, two_ref, cut_one_ref, cut_two_ref, load_sem, store_sem,
):
    _, _, blocks, width, _, _, vecs, kept, _ = cfg
    span_one = kept + vecs
    span_two = span_one + vecs
    pieces = 4
    step = 4
    chunks = blocks // step // pieces
    span = chunks * step * width
    loads = []
    for piece in range(pieces):
        part = pl.ds(piece * span, span)
        for n, (src, start, count) in enumerate([
            (basis_hbm.at[0], 0, kept), (vec_hbm.at[0], kept, vecs),
            (one_in_hbm, span_one, vecs), (image_hbm, span_two, vecs)]):
            loads.append(pltpu.make_async_copy(
                src.at[:, part], work_ref.at[pl.ds(start, count), part], load_sem.at[piece, n]))
            loads[-1].start()
    cut_one_ref[...] = small_ref[pl.ds(0, vecs), :span_one + vecs]
    cut_two_ref[...] = small_ref[pl.ds(vecs, vecs), :span_two + vecs]
    stores = [
        pltpu.make_async_copy(cut_one_ref, coef_one_hbm, store_sem.at[0]),
        pltpu.make_async_copy(cut_two_ref, coef_two_hbm, store_sem.at[1])]
    for copy in stores:
        copy.start()
    spread(small_ref[pl.ds(2 * vecs, vecs), :], bcast_ref, vecs + span_two, vecs, width)
    step, body = combine(
        work_ref, bcast_ref, span_two, list(range(span_two)), vecs, width, two_ref, None)
    for piece in range(pieces):
        part = pl.ds(piece * span, span)
        for copy in loads[4 * piece:4 * piece + 4]:
            copy.wait()
        stores.append(pltpu.make_async_copy(
            work_ref.at[pl.ds(span_one, vecs), part], one_hbm.at[0, :, part],
            store_sem.at[2 + piece]))
        stores[-1].start()
        lax.fori_loop(piece * chunks, (piece + 1) * chunks, body, 0)
        stores.append(pltpu.make_async_copy(
            two_ref.at[:, part], two_hbm.at[0, :, part], store_sem.at[2 + pieces + piece]))
        stores[-1].start()
    for copy in stores:
        copy.wait()


def per_device(
    vectors, basis, potential, hop_table, soc_table, nbr_block, nbr_type, nbr_count, flip_block
):
    blocks, slots = nbr_block.shape
    types, width, _ = hop_table.shape
    vecs, kept = vectors.shape[1], basis.shape[1]
    dom_total = lax.axis_size("dom")
    group_doms = 4 if dom_total % 4 == 0 else 1
    groups = dom_total // group_doms
    reach = blocks + 2 * RANGE
    norm = float(2 * blocks * width * dom_total)
    cfg = (dom_total, group_doms, blocks, width, types, slots, vecs, kept, norm)
    count = blocks * width
    rows = blocks * vecs
    span_one, span_two = kept + vecs, kept + 2 * vecs
    vmem = pl.BlockSpec(memory_space=pltpu.VMEM)
    hbm = pl.BlockSpec(memory_space=pltpu.HBM)
    f32, bf16, i32 = jnp.float32, jnp.bfloat16, jnp.int32
    dma = pltpu.SemaphoreType.DMA
    shape = jax.ShapeDtypeStruct
    limit = 64 * 1000 * 1000
    one, image, small = pl.pallas_call(
        functools.partial(kernel, cfg),
        name="krylov",
        out_shape=(
            shape((vecs, count), f32),
            shape((vecs, count), f32),
            shape((3 * vecs, width), f32),
        ),
        in_specs=[hbm] * 9,
        out_specs=(hbm, hbm, vmem),
        scratch_shapes=[
            pltpu.VMEM((span_two + vecs, count), f32),
            pltpu.VMEM((span_two + vecs, vecs, width), f32),
            pltpu.VMEM((1, count), f32),
            pltpu.VMEM((types * width, width), bf16),
            pltpu.VMEM(soc_table.shape, bf16),
            pltpu.VMEM((slots, blocks), i32),
            pltpu.VMEM((slots, blocks), i32),
            pltpu.VMEM((1, blocks), i32),
            pltpu.VMEM((1, blocks), i32),
            pltpu.VMEM((blocks, width), i32),
            pltpu.SMEM((blocks, width), i32),
            pltpu.VMEM((2, rows, width), bf16),
            pltpu.VMEM((2, rows, width), bf16),
            pltpu.VMEM((2, 2 * RANGE * vecs, width), bf16),
            pltpu.VMEM((reach * types + 1 + blocks, vecs, width), f32),
            pltpu.VMEM((2, 2 * group_doms, vecs, width), f32),
            pltpu.VMEM((2, groups, vecs, width), f32),
            dma((12,)),
            dma((2, 3)), dma((2, 3)),
            dma((2, 2 * group_doms)), dma((2, 2 * group_doms)),
            dma((2, groups)), dma((2, groups)),
        ],
        compiler_params=pltpu.CompilerParams(
            collective_id=0, has_side_effects=True, vmem_limit_bytes=limit),
    )(
        vectors, basis, potential, hop_table.reshape(types * width, width), soc_table,
        nbr_block.T, nbr_type.T, nbr_count.reshape(1, blocks), flip_block.reshape(1, blocks))
    one, two, coef_one, coef_two = pl.pallas_call(
        functools.partial(finish, cfg),
        name="finish",
        out_shape=(
            shape((1, vecs, count), f32),
            shape((1, vecs, count), f32),
            shape((vecs, span_one + vecs), f32),
            shape((vecs, span_two + vecs), f32),
        ),
        in_specs=[vmem] + [hbm] * 4,
        out_specs=(hbm,) * 4,
        scratch_shapes=[
            pltpu.VMEM((span_two + vecs, count), f32),
            pltpu.VMEM((span_two + vecs, vecs, width), f32),
            pltpu.VMEM((vecs, count), f32),
            pltpu.VMEM((vecs, span_one + vecs), f32),
            pltpu.VMEM((vecs, span_two + vecs), f32),
            dma((4, 4)), dma((10,)),
        ],
        compiler_params=pltpu.CompilerParams(vmem_limit_bytes=limit),
    )(small, vectors, basis, one, image)
    return one, two, coef_one.T, coef_two.T


def solution(mesh):
    return jax.shard_map(
        per_device,
        mesh=mesh,
        in_specs=(
            P("spin", None, "dom"),
            P("spin", None, "dom"),
            P("spin", "dom"),
            P(),
            P(),
            P("dom", None),
            P("dom", None),
            P("dom"),
            P("dom"),
        ),
        out_specs=(P("spin", None, "dom"), P("spin", None, "dom"), P(), P()),
        check_vma=False,
    )
```
